32 devices in a mesh: dp: 1, seq: 32 (over z, y, x, core).
Axes of the slice: x: 2, y: 2, z: 4, core: 2. Of those that a mesh axis runs over, the one named last changes fastest.
Arguments:
- waveform: float32 [1, 163840], P('dp', 'seq'), may hold values from -45 to 45
- lengths: int32 [1, 4], P('dp'), may hold values from 1 to 30, 60 in all within a row
- conv_first: float32 [10, 512], replicated, may hold values from -2 to 2
- conv_second: bfloat16 [1536, 512], replicated, may hold values from -0.15625 to 0.15625
- cotangent: bfloat16 [1, 16384, 512], P('dp', 'seq'), may hold values from -6 to 6
Outputs:
- features: bfloat16 [1, 16384, 512], P('dp', 'seq')
- grad_first: float32 [10, 512], replicated
- grad_second: float32 [1536, 512], replicated
The draws below stay inside these ranges and needn't reach their ends.
All inputs are finite; a program needn't handle non-finite values.
Results may differ from the reference program's by a relative error of at most 0.001.
The reference program's roundings to bfloat16 on the way (of `first_out` and `second_delta`) count: a program that leaves them out, or rounds other values in their place, can miss the bound.
Values sent between devices are 32-bit elements; how exact they have to be, the bound alone decides.
A program may use at most 64 MiB of HBM per device.

```python
import math
import jax
import jax.numpy as jnp
import numpy as np
from jax import lax

C = 512
UTTS = 4
MIN_UNITS = 50
GROUPS = 1
SAMPLES = 163840
FRAMES1 = 16384
DRAW_TOTAL = 60
DRAW_MOST = 30


def draw_waveform(key, part):
    key_base = jax.random.fold_in(key, 11)
    key_env = jax.random.fold_in(key, 23)
    places = jnp.arange(SAMPLES, dtype=jnp.float32) / float(SAMPLES)
    ramp = 1.0 + 2.0 * places
    envelope = jnp.exp(jax.random.uniform(key_env, (GROUPS, SAMPLES // 160), minval=0.0, maxval=math.log(10.0)))
    envelope = jnp.repeat(envelope, 160, axis=1)
    base = jnp.clip(jax.random.normal(key_base, (GROUPS, SAMPLES)), -5.0, 5.0)
    return (0.3 * base * envelope * ramp[None, :]).astype(jnp.float32)


def block_scale(own_key, shape, split, low, largest):
    gain, own = 1.0, jax.random.fold_in(own_key, 6)
    for axis_at, shards_of in split:
        draws = jnp.exp(jax.random.uniform(jax.random.fold_in(own, axis_at), (shards_of,), jnp.float32, low / len(split), largest / len(split)))
        gain = gain * jnp.repeat(draws, shape[axis_at] // shards_of).reshape([-1 if axis == axis_at else 1 for axis in range(len(shape))])
    return gain


def profile(number_of, total, limit, slope):
    loads = [(1 << 20) // math.isqrt(rank ** slope) + 1 for rank in range(2, number_of + 1)]
    surplus, given = total - limit - (number_of - 1), [1] * (number_of - 1)
    while surplus > 0:
        movable = [i for i in range(number_of - 1) if given[i] < limit]
        whole, budget = sum([loads[i] for i in movable]), surplus
        for i in movable:
            addition = min(limit - given[i], max(1, budget * loads[i] // whole), surplus)
            given[i] = given[i] + addition
            surplus = surplus - addition
    return np.array([limit] + given)


def uneven(stream_key, amount, total, most, lean):
    if amount == 2:
        one = jax.random.randint(stream_key, (), max(1, total - most), min(most, total - 1) + 1)
        return jnp.stack([one, total - one])
    sizes = jnp.asarray(profile(amount, total, most, lean), jnp.int32)
    pairs = (amount - 1) // 2
    donor, sink = sizes[1:1 + 2 * pairs:2], sizes[2:2 + 2 * pairs:2]
    margin = jnp.minimum(donor - 1, most - sink)
    passed = jax.random.randint(jax.random.fold_in(stream_key, 1), (pairs,), 0, 1 << 20) % (margin + 1)
    sizes = sizes.at[1:1 + 2 * pairs:2].set(donor - passed).at[2:2 + 2 * pairs:2].set(sink + passed)
    return sizes[jax.random.permutation(jax.random.fold_in(stream_key, 2), amount)]


def scatter_about(rng, extent, deviation, bound, pieces=(), held_as=jnp.bfloat16):
    gain = block_scale(rng, extent, pieces, -0.22, 0.18) if pieces else 1.0
    result = jax.random.normal(rng, extent, jnp.float32) * deviation * gain
    return jnp.minimum(jnp.maximum(result, -bound), bound).astype(held_as)


def setup_inputs(seed: int = 0) -> dict:
    arg_keys = jax.random.split(jax.random.key(seed), 6)
    waveform = draw_waveform(jax.random.fold_in(arg_keys[5], 71), 0)
    lengths = jax.vmap(lambda own: uneven(own, UTTS, DRAW_TOTAL, DRAW_MOST, 2))(jax.random.split(arg_keys[1], GROUPS)).reshape((GROUPS, UTTS)).astype(jnp.int32)
    conv_first = scatter_about(arg_keys[2], (10, C), 10 ** -0.5, 2.0, (), jnp.float32)
    conv_second = scatter_about(arg_keys[3], (3 * C, C), (3 * C) ** -0.5, 0.15625)
    cotangent = scatter_about(arg_keys[4], (GROUPS, FRAMES1, C), 1.0, 6.0, ((1, 32),))
    return {"waveform": waveform, "lengths": lengths, "conv_first": conv_first, "conv_second": conv_second, "cotangent": cotangent}


HIGH = lax.Precision.HIGHEST

def gelu_exact(value):
    return 0.5 * value * (1.0 + lax.erf(value * 0.7071067811865476))

def gelu_slope(value):
    return 0.5 * (1.0 + lax.erf(value * 0.7071067811865476)) + value * jnp.exp(-0.5 * value * value) * 0.3989422804014327

def frame_info(lengths_row, first_sample, frame_count, stride):
    utt_units = lengths_row + (MIN_UNITS - 1)
    utt_ends = jnp.cumsum(utt_units, dtype=jnp.int32) * 640
    starts = utt_ends - utt_units * 640
    places = first_sample + stride * jnp.arange(frame_count, dtype=jnp.int32)
    inside = (places[:, None] >= starts[None, :]) & (places[:, None] < utt_ends[None, :])
    end_of = lax.optimization_barrier(jnp.sum(jnp.where(inside, utt_ends[None, :], 0), axis=1, dtype=jnp.int32))
    counts = (utt_units * 128 - 1).astype(jnp.float32)
    return (inside.astype(jnp.float32), places, end_of, counts)

def first_layer(extended, conv_first, frame_count):
    blocks = extended[:5 * (frame_count + 1)].reshape(frame_count + 1, 5)
    patches = jnp.concatenate([blocks[:-1], blocks[1:]], axis=1)
    return (patches, jnp.dot(patches, conv_first, precision=HIGH, preferred_element_type=jnp.float32))

def second_rows(first_out, frame_count):
    pairs = first_out[:frame_count].reshape(frame_count // 2, 2 * first_out.shape[1])
    third = first_out[2:frame_count + 1:2]
    return jnp.concatenate([pairs, third], axis=1)

def spread_back(slopes, frame_count, channels):
    near_part = slopes[:, :2 * channels].reshape(frame_count, channels)
    far_part = slopes[:, 2 * channels:]
    spread = jnp.stack([far_part, jnp.zeros_like(far_part)], axis=1).reshape(frame_count, channels)
    padded = jnp.concatenate([jnp.zeros((2, channels), slopes.dtype), spread], axis=0)
    return (near_part + padded[:frame_count], padded[frame_count:frame_count + 1])

def replica_pass(samples, lengths_row, conv_first, conv_second, cot_rows):
    frame_count = samples.shape[0] // 5
    out_count = frame_count // 2
    channels = conv_second.shape[1]
    extended = jnp.concatenate([samples, jnp.zeros((10,), samples.dtype)])
    patches, first_pre = first_layer(extended, conv_first, frame_count + 1)
    member, places, end_of, counts = frame_info(lengths_row, 0, frame_count + 1, 5)
    first_valid = (places + 10 <= end_of).astype(jnp.float32)[:, None]
    own_member = member[:frame_count]
    own_pre = first_pre[:frame_count] * first_valid[:frame_count]
    sum_one = jnp.dot(own_member.T, own_pre, precision=HIGH)
    sum_two = jnp.dot(own_member.T, own_pre * first_pre[:frame_count], precision=HIGH)
    utt_mean = sum_one / counts[:, None]
    utt_var = sum_two / counts[:, None] - utt_mean * utt_mean
    utt_rstd = lax.rsqrt(utt_var + 1e-05)
    frame_mean = jnp.dot(member, utt_mean, precision=HIGH)
    frame_rstd = jnp.dot(member, utt_rstd, precision=HIGH)
    first_norm = (first_pre - frame_mean) * frame_rstd
    first_out = (gelu_exact(first_norm) * first_valid).astype(jnp.bfloat16)
    rows_second = second_rows(first_out, frame_count)
    second_pre = jnp.dot(rows_second, conv_second, preferred_element_type=jnp.float32)
    out_member, out_places, out_end, out_counts = frame_info(lengths_row, 0, out_count, 10)
    second_valid = (out_places + 20 <= out_end).astype(jnp.float32)[:, None]
    features = (gelu_exact(second_pre) * second_valid).astype(jnp.bfloat16)
    second_delta = (cot_rows.astype(jnp.float32) * second_valid * gelu_slope(second_pre)).astype(jnp.bfloat16)
    grad_second = jnp.dot(rows_second.T, second_delta, preferred_element_type=jnp.float32)
    slopes = jnp.dot(second_delta, conv_second.T, preferred_element_type=jnp.float32)
    first_delta, dropped = spread_back(slopes, frame_count, channels)
    own_valid = first_valid[:frame_count]
    own_norm = first_norm[:frame_count]
    norm_delta = first_delta * gelu_slope(own_norm) * own_valid
    back_one = jnp.dot(own_member.T, norm_delta, precision=HIGH) / counts[:, None]
    back_two = jnp.dot(own_member.T, norm_delta * own_norm, precision=HIGH) / counts[:, None]
    pre_delta = frame_rstd[:frame_count] * own_valid * (norm_delta - jnp.dot(own_member, back_one, precision=HIGH) - own_norm * jnp.dot(own_member, back_two, precision=HIGH))
    grad_first = jnp.dot(patches[:frame_count].T, pre_delta, precision=HIGH)
    return (features, grad_first, grad_second)

def reference(waveform, lengths, conv_first, conv_second, cotangent):
    outputs = []
    total_first = jnp.zeros(conv_first.shape, jnp.float32)
    total_second = jnp.zeros(conv_second.shape, jnp.float32)
    for replica in range(GROUPS):
        features, grad_first, grad_second = replica_pass(waveform[replica], lengths[replica], conv_first, conv_second, cotangent[replica])
        outputs.append(features)
        total_first = total_first + grad_first
        total_second = total_second + grad_second
    factor = float(GROUPS * FRAMES1) ** (-0.5)
    return (jnp.stack(outputs, axis=0), total_first * factor, total_second * factor)
```

```python
import functools

import jax
import jax.numpy as jnp
from jax import lax
from jax.experimental import pallas as pl
from jax.experimental.pallas import tpu as pltpu
from jax.sharding import PartitionSpec as P

MIN_UNITS = 50
TAPS = 10
HIGH = lax.Precision.HIGHEST
MESH = pl.DeviceIdType.MESH
F32 = jnp.float32
BLOCK = 64


def dot_tn(a, b, precision=None):
    return lax.dot_general(
        a, b, (((0,), (0,)), ((), ())), precision=precision, preferred_element_type=F32
    )


def dot_nt(a, b):
    return lax.dot_general(a, b, (((1,), (1,)), ((), ())), preferred_element_type=F32)


def stage_orders(bits):
    if bits != 5:
        return [list(range(bits))] * 4
    return [[0, 1, 2, 3, 4], [0, 2, 3, 1, 4], [0, 3, 1, 2, 4], [0, 1, 2, 3, 4]]


class Part:
    def __init__(self, me, order, src, inbox, out, size, send_sems, recv_sems):
        self.me, self.order, self.src, self.inbox, self.out = me, order, src, inbox, out
        self.send_sems, self.recv_sems = send_sems, recv_sems
        self.stages = len(order)
        self.size, self.off, self.room, self.at = size, 0, 0, 0
        self.copies = []

    def bit(self, stage):
        return (self.me // (1 << self.order[stage])) % 2

    def send(self, src, dst, stage, number):
        partner = self.me + (1 - 2 * self.bit(stage)) * (1 << self.order[stage])
        copy = pltpu.make_async_remote_copy(
            src_ref=src,
            dst_ref=dst,
            send_sem=self.send_sems.at[number],
            recv_sem=self.recv_sems.at[number],
            device_id={"seq": partner},
            device_id_type=MESH,
        )
        copy.start()
        self.copies.append(copy)

    def start(self):
        if self.at < self.stages:
            half = self.size // 2
            bit = self.bit(self.at)
            self.send(
                self.src.at[pl.ds(self.off + (1 - bit) * half, half)],
                self.inbox.at[pl.ds(self.room, half)],
                self.at,
                self.at,
            )
            self.off = self.off + bit * half
            self.size = half
        elif self.at < 2 * self.stages:
            own = self.out.at[pl.ds(self.off, self.size)]
            self.send(own, own, 2 * self.stages - 1 - self.at, self.at)

    def finish(self):
        self.copies[self.at].wait_recv()
        if self.at < self.stages:
            last = self.at == self.stages - 1
            target = self.out if last else self.src
            step = min(self.size, 16)

            def add(i, carry):
                here = pl.ds(self.off + i * step, step)
                target[here] = self.src[here] + self.inbox[pl.ds(self.room + i * step, step)]
                return carry

            lax.fori_loop(0, self.size // step, add, 0)
            self.room += self.size
        else:
            bit = self.bit(2 * self.stages - 1 - self.at)
            self.off = self.off - bit * self.size
            self.size = self.size * 2
        self.at += 1

    def step(self):
        self.finish()
        self.start()

    def drain(self):
        for copy in self.copies:
            copy.wait_send()


def kernel(
    n, factor,
    lengths_ref, taps_ref, first_ref, second_ref, cot_ref,
    feat_ref, grad1_ref, grad2_ref,
    norm_ref, slope_ref, q_ref, x_ref, sd_ref,
    slots_a, slots_b, buf, inbox, outb, ex, ex_in, ex_out, erow,
    send_sems, recv_sems, stat_send, stat_recv,
):
    me = lax.axis_index("seq")
    rows = sd_ref.shape[0]
    channels = first_ref.shape[1]
    utts = lengths_ref.shape[1]
    bits = n.bit_length() - 1
    low = min(3, bits)
    group = 1 << low
    groups = n // group
    my_low, my_high = me % group, me // group
    first_sample = me * (rows * TAPS)

    barrier = pltpu.get_barrier_semaphore()
    orders = stage_orders(bits)

    def flip(mask):
        out = me
        for b in range(bits):
            if mask >> b & 1:
                out = out + (1 - 2 * ((me // (1 << b)) % 2)) * (1 << b)
        return out

    stat_masks = list(range(1, group)) + [k * group for k in range(1, groups)]
    all_masks = sorted(set(stat_masks) | {1 << b for b in range(bits)})
    for mask in all_masks:
        pl.semaphore_signal(
            barrier, inc=1, device_id={"seq": flip(mask)}, device_id_type=MESH
        )

    units = [lengths_ref[0, u] + (MIN_UNITS - 1) for u in range(utts)]
    ends, total = [], jnp.int32(0)
    for u in range(utts):
        total = total + units[u] * 640
        ends.append(total)
    here = jnp.int32(0)
    for u in range(utts - 1):
        here = here + jnp.where(first_sample >= ends[u], 1, 0)
    end_a, end_b = jnp.int32(0), jnp.int32(0)
    for u in range(utts):
        end_a = jnp.where(here == u, ends[u], end_a)
        end_b = jnp.where(here + 1 == u, ends[u], end_b)

    def masks(t, start, count, width):
        row = lax.broadcasted_iota(jnp.int32, (count, width), 0) + start
        place = first_sample + 5 * t + TAPS * row
        is_b = place >= end_a
        valid = place + TAPS <= jnp.where(is_b, end_b, end_a)
        return is_b, valid

    lane = lax.broadcasted_iota(jnp.int32, (BLOCK, 128), 1)
    lane_b = ((lane >= 16) & (lane < 32)) | (lane == 33)

    zero_row = jnp.zeros((1, channels), F32)
    sq = (zero_row, zero_row)
    for t in range(3):
        def conv_block(i, carry, t=t):
            start = pl.multiple_of(i * BLOCK, BLOCK)
            at = pl.ds(pl.multiple_of(t * rows + i * BLOCK, BLOCK), BLOCK)
            taps = taps_ref[at]
            pre = jnp.dot(taps, first_ref[...], precision=HIGH, preferred_element_type=F32)
            norm_ref[at] = pre
            is_b, valid = masks(t, start, BLOCK, 128)
            q_ref[at] = jnp.where(valid & (is_b == lane_b), taps, 0.0)
            if t == 2:
                return carry
            is_b, valid = masks(t, start, BLOCK, channels)
            square = jnp.where(valid, pre * pre, 0.0)
            in_b = jnp.where(is_b, square, 0.0)
            in_a = jnp.where(is_b, 0.0, square)
            return (
                carry[0] + jnp.sum(in_a, axis=0, keepdims=True),
                carry[1] + jnp.sum(in_b, axis=0, keepdims=True),
            )

        sq = lax.fori_loop(0, rows // BLOCK, conv_block, sq)
    both = pl.ds(0, 2 * rows)
    sums = dot_tn(q_ref[both], norm_ref[both], HIGH)

    def spread(a, b):
        return [
            jnp.where(here == u, a, jnp.where(here + 1 == u, b, jnp.zeros_like(a)))
            for u in range(utts)
        ]

    stats = spread(sums[32:33], sums[33:34]) + spread(sq[0], sq[1])
    slots_a[my_low] = jnp.concatenate(stats, axis=0)
    pl.semaphore_wait(barrier, len(all_masks))

    def exchange(slots, mine, members, number):
        copies = []
        for i, mask in enumerate(members):
            copy = pltpu.make_async_remote_copy(
                src_ref=slots.at[mine],
                dst_ref=slots.at[mine],
                send_sem=stat_send.at[number + i],
                recv_sem=stat_recv.at[number + i],
                device_id={"seq": flip(mask)},
                device_id_type=MESH,
            )
            copy.start()
            copies.append(copy)
        return copies

    stat_copies = exchange(slots_a, my_low, range(1, group), 0)
    qq = dot_tn(q_ref[both], q_ref[both], HIGH)
    for copy in stat_copies:
        copy.wait_recv()
    total = slots_a[0]
    for i in range(1, group):
        total = total + slots_a[i]
    if groups > 1:
        slots_b[my_high] = total
        more = exchange(slots_b, my_high, [k * group for k in range(1, groups)], group - 1)
        for copy in more:
            copy.wait_recv()
        stat_copies = stat_copies + more
        total = slots_b[0]
        for i in range(1, groups):
            total = total + slots_b[i]
    means, rstds, inverse = [], [], []
    for u in range(utts):
        count = jnp.full((1, channels), units[u] * 128 - 1, jnp.int32).astype(F32)
        mean = total[u : u + 1] / count
        var = total[utts + u : utts + u + 1] / count - mean * mean
        means.append(mean)
        rstds.append(lax.rsqrt(var + 1e-05))
        inverse.append(count)

    def pick(values, offset):
        out = zero_row
        for u in range(utts):
            out = jnp.where(here + offset == u, values[u], out)
        return out

    mean_a, mean_b = pick(means, 0), pick(means, 1)
    rstd_a, rstd_b = pick(rstds, 0), pick(rstds, 1)

    for t in range(3):
        def gelu_block(i, carry, t=t):
            start = pl.multiple_of(i * 32, 32)
            at = pl.ds(pl.multiple_of(t * rows + i * 32, 32), 32)
            is_b, valid = masks(t, start, 32, channels)
            norm = (norm_ref[at] - jnp.where(is_b, mean_b, mean_a)) * jnp.where(
                is_b, rstd_b, rstd_a
            )
            norm_ref[at] = norm
            cdf = 0.5 * (1.0 + lax.erf(norm * 0.7071067811865476))
            x_ref[at] = jnp.where(valid, norm * cdf, 0.0).astype(jnp.bfloat16)
            slope = cdf + norm * jnp.exp(-0.5 * norm * norm) * 0.3989422804014327
            slope_ref[at] = jnp.where(valid, slope, 0.0)
            return carry

        lax.fori_loop(0, rows // 32, gelu_block, 0)

    def second_block(i, carry):
        start = pl.multiple_of(i * 128, 128)
        pre = jnp.zeros((128, channels), F32)
        for t in range(3):
            pre = pre + jnp.dot(
                x_ref[pl.ds(pl.multiple_of(t * rows + i * 128, 128), 128)],
                second_ref[t * channels : (t + 1) * channels],
                preferred_element_type=F32,
            )
        row = lax.broadcasted_iota(jnp.int32, (128, channels), 0) + start
        place = first_sample + TAPS * row
        valid = place + 2 * TAPS <= jnp.where(place >= end_a, end_b, end_a)
        cdf = 0.5 * (1.0 + lax.erf(pre * 0.7071067811865476))
        at = pl.ds(start, 128)
        feat_ref[at] = jnp.where(valid, pre * cdf, 0.0).astype(jnp.bfloat16)
        slope = cdf + pre * jnp.exp(-0.5 * pre * pre) * 0.3989422804014327
        sd_ref[at] = jnp.where(valid, cot_ref[at].astype(F32) * slope, 0.0).astype(jnp.bfloat16)
        return carry

    lax.fori_loop(0, rows // 128, second_block, 0)

    blocks = channels // 128
    tall = channels // 8
    size = blocks * tall
    parts = []
    for t in range(3):
        part = Part(
            me, orders[t], buf.at[pl.ds(t * size, size)], inbox.at[pl.ds(t * size, size)],
            outb.at[pl.ds(t * size, size)], size, send_sems.at[t], recv_sems.at[t],
        )
        grad = dot_tn(x_ref[t * rows : (t + 1) * rows], sd_ref[...])
        for c in range(blocks):
            buf[t * size + c * tall : t * size + (c + 1) * tall] = grad[
                :, c * 128 : (c + 1) * 128
            ].reshape(tall, 8, 128)
        part.start()
        parts.append(part)

    back = (zero_row, zero_row, zero_row, zero_row)
    for t in range(3):
        weight = second_ref.at[t * channels : (t + 1) * channels]

        def back_block(i, carry, t=t, weight=weight):
            start = pl.multiple_of(i * BLOCK, BLOCK)
            at = pl.ds(pl.multiple_of(t * rows + i * BLOCK, BLOCK), BLOCK)
            delta = dot_nt(sd_ref[pl.ds(start, BLOCK)], weight[...]) * slope_ref[at]
            slope_ref[at] = delta
            is_b, _ = masks(t, start, BLOCK, channels)
            scaled = delta * norm_ref[at]
            add = [jnp.where(is_b, 0.0, delta), jnp.where(is_b, delta, 0.0)]
            add += [jnp.where(is_b, 0.0, scaled), jnp.where(is_b, scaled, 0.0)]
            return tuple(c + jnp.sum(a, axis=0, keepdims=True) for c, a in zip(carry, add))

        back = lax.fori_loop(0, rows // BLOCK, back_block, back)
    for part in parts:
        part.step()
    acc = dot_tn(q_ref[...], slope_ref[...], HIGH)

    grad_a = rstd_a * acc[0:16] + rstd_b * acc[16:32]
    erow[0:16] = grad_a
    one = spread(back[0], back[1])
    two = spread(back[2], back[3])
    erow[16:24] = jnp.concatenate(one + two, axis=0)
    norm_a = rstd_a * (sums[0:16] - qq[0:16, 32:33] * mean_a)
    norm_b = rstd_b * (sums[16:32] - qq[16:32, 33:34] * mean_b)
    per = spread(norm_a, norm_b)
    for u in range(utts):
        erow[24 + u * TAPS : 24 + (u + 1) * TAPS] = per[u][:TAPS]
    for u, w in enumerate(spread(qq[32:33], qq[33:34])):
        erow[10 + u : 11 + u, 0:128] = w
    high = erow.shape[0] // 8
    for c in range(blocks):
        ex[c * high : (c + 1) * high] = erow[:, c * 128 : (c + 1) * 128].reshape(high, 8, 128)
    extra = Part(
        me, orders[3], ex, ex_in, ex_out, blocks * high, send_sems.at[3], recv_sems.at[3]
    )
    extra.start()
    for _ in range(2 * bits - 1):
        for part in parts:
            part.step()
        extra.step()
    extra.finish()
    for t in range(3):
        for c in range(blocks):
            grad2_ref[t * channels : (t + 1) * channels, c * 128 : (c + 1) * 128] = (
                outb[t * size + c * tall : t * size + (c + 1) * tall].reshape(channels, 128) * factor
            )
    for c in range(blocks):
        erow[:, c * 128 : (c + 1) * 128] = ex_out[c * high : (c + 1) * high].reshape(8 * high, 128)
    weights, scales = [], []
    result = erow[0:TAPS]
    for u in range(utts):
        weights.append(erow[10 + u : 11 + u, 0:128])
        scales.append(rstds[u] * (erow[16 + u : 17 + u] / inverse[u]))
        result = result - rstds[u] * (erow[16 + utts + u : 17 + utts + u] / inverse[u]) * (
            erow[24 + u * TAPS : 24 + (u + 1) * TAPS]
        )
    pad = [jnp.zeros((8 - utts, 128), F32)], [jnp.zeros((8 - utts, channels), F32)]
    plain = dot_tn(
        jnp.concatenate(weights + pad[0], axis=0), jnp.concatenate(scales + pad[1], axis=0), HIGH
    )
    grad1_ref[...] = (result - plain[0:TAPS] - plain[16 : 16 + TAPS]) * factor
    for copy in stat_copies:
        copy.wait_send()
    for part in parts + [extra]:
        part.drain()


def on_device(waveform, lengths, conv_first, conv_second, cotangent):
    n = lax.axis_size("seq")
    samples = waveform[0]
    rows = samples.shape[0] // TAPS
    channels = conv_second.shape[1]
    utts = lengths.shape[1]
    assert 24 + utts * TAPS <= 64 and utts == 4 and samples.shape[0] < MIN_UNITS * 640
    ahead = lax.ppermute(samples[:TAPS], "seq", [(i, i - 1) for i in range(1, n)])
    table = jnp.concatenate([samples, ahead]).reshape(rows + 1, TAPS)
    middle = jnp.concatenate([table[:-1, 5:], table[1:, :5]], axis=1)
    taps = jnp.concatenate([table[:-1], middle, table[1:]], axis=0)
    count = 3 * rows
    gap = jnp.zeros((count, 6), F32)
    taps = jnp.concatenate(
        [taps, gap, taps, gap, jnp.ones((count, 2), F32), jnp.zeros((count, 94), F32)], axis=1
    )
    first = jnp.concatenate([conv_first, jnp.zeros((128 - TAPS, channels), F32)], axis=0)
    factor = float(lax.axis_size("dp") * rows * n) ** (-0.5)
    tiles = 3 * channels // 8 * (channels // 128)
    small = 64 // 8 * (channels // 128)
    bits = n.bit_length() - 1
    vmem = pl.BlockSpec(memory_space=pltpu.VMEM)
    feats, grad1, grad2 = pl.pallas_call(
        functools.partial(kernel, n, factor),
        name="encoder",
        out_shape=(
            jax.ShapeDtypeStruct((rows, channels), jnp.bfloat16),
            jax.ShapeDtypeStruct((TAPS, channels), F32),
            jax.ShapeDtypeStruct((3 * channels, channels), F32),
        ),
        in_specs=[pl.BlockSpec(memory_space=pltpu.SMEM)] + [vmem] * 4,
        out_specs=(vmem, vmem, vmem),
        scratch_shapes=[
            pltpu.VMEM((count, channels), F32),
            pltpu.VMEM((count, channels), F32),
            pltpu.VMEM((count, 128), F32),
            pltpu.VMEM((count, channels), jnp.bfloat16),
            pltpu.VMEM((rows, channels), jnp.bfloat16),
            pltpu.VMEM((8, 2 * utts, channels), F32),
            pltpu.VMEM((max(1, n // 8), 2 * utts, channels), F32),
            pltpu.VMEM((tiles, 8, 128), F32),
            pltpu.VMEM((tiles, 8, 128), F32),
            pltpu.VMEM((tiles, 8, 128), F32),
            pltpu.VMEM((small, 8, 128), F32),
            pltpu.VMEM((small, 8, 128), F32),
            pltpu.VMEM((small, 8, 128), F32),
            pltpu.VMEM((64, channels), F32),
            pltpu.SemaphoreType.DMA((4, 2 * bits)),
            pltpu.SemaphoreType.DMA((4, 2 * bits)),
            pltpu.SemaphoreType.DMA((8 + n // 8,)),
            pltpu.SemaphoreType.DMA((8 + n // 8,)),
        ],
        compiler_params=pltpu.CompilerParams(
            collective_id=0, has_side_effects=True, vmem_limit_bytes=60 * 1024 * 1024
        ),
    )(lengths, taps, first, conv_second, cotangent[0])
    if lax.axis_size("dp") > 1:
        grad1, grad2 = lax.psum((grad1, grad2), "dp")
    return (feats[None], grad1, grad2)


def solution(mesh):
    placed = (P("dp", "seq"), P("dp", None), P(), P(), P("dp", "seq", None))
    return jax.shard_map(
        on_device,
        mesh=mesh,
        in_specs=placed,
        out_specs=(P("dp", "seq", None), P(), P()),
        check_vma=False,
    )
```

```python
import functools

import jax
import jax.numpy as jnp
from jax import lax
from jax.experimental import pallas as pl
from jax.experimental.pallas import tpu as pltpu
from jax.sharding import PartitionSpec as P

MIN_UNITS = 50
TAPS = 10
HIGH = lax.Precision.HIGHEST
MESH = pl.DeviceIdType.MESH
F32 = jnp.float32
BLOCK = 64


def dot_tn(a, b, precision=None):
    return lax.dot_general(
        a, b, (((0,), (0,)), ((), ())), precision=precision, preferred_element_type=F32
    )


def dot_nt(a, b):
    return lax.dot_general(a, b, (((1,), (1,)), ((), ())), preferred_element_type=F32)


def stage_orders(bits):
    if bits != 5:
        return [list(range(bits))] * 4
    return [[0, 1, 2, 3, 4], [0, 2, 3, 1, 4], [0, 3, 1, 2, 4], [0, 1, 2, 3, 4]]


class Part:
    def __init__(self, me, order, src, inbox, out, size, send_sems, recv_sems):
        self.me, self.order, self.src, self.inbox, self.out = me, order, src, inbox, out
        self.send_sems, self.recv_sems = send_sems, recv_sems
        self.stages = len(order)
        self.size, self.off, self.room, self.at = size, 0, 0, 0
        self.copies = []

    def bit(self, stage):
        return (self.me // (1 << self.order[stage])) % 2

    def send(self, src, dst, stage, number):
        partner = self.me + (1 - 2 * self.bit(stage)) * (1 << self.order[stage])
        copy = pltpu.make_async_remote_copy(
            src_ref=src,
            dst_ref=dst,
            send_sem=self.send_sems.at[number],
            recv_sem=self.recv_sems.at[number],
            device_id={"seq": partner},
            device_id_type=MESH,
        )
        copy.start()
        self.copies.append(copy)

    def start(self):
        if self.at < self.stages:
            half = self.size // 2
            bit = self.bit(self.at)
            self.send(
                self.src.at[pl.ds(self.off + (1 - bit) * half, half)],
                self.inbox.at[pl.ds(self.room, half)],
                self.at,
                self.at,
            )
            self.off = self.off + bit * half
            self.size = half
        elif self.at < 2 * self.stages:
            own = self.out.at[pl.ds(self.off, self.size)]
            self.send(own, own, 2 * self.stages - 1 - self.at, self.at)

    def finish(self):
        self.copies[self.at].wait_recv()
        if self.at < self.stages:
            last = self.at == self.stages - 1
            target = self.out if last else self.src
            step = min(self.size, 16)

            def add(i, carry):
                here = pl.ds(self.off + i * step, step)
                target[here] = self.src[here] + self.inbox[pl.ds(self.room + i * step, step)]
                return carry

            lax.fori_loop(0, self.size // step, add, 0)
            self.room += self.size
        else:
            bit = self.bit(2 * self.stages - 1 - self.at)
            self.off = self.off - bit * self.size
            self.size = self.size * 2
        self.at += 1

    def step(self):
        self.finish()
        self.start()

    def drain(self):
        for copy in self.copies:
            copy.wait_send()


def kernel(
    n, factor,
    lengths_ref, wave_ref, conv_ref, second_ref, cot_ref,
    feat_ref, grad1_ref, outb,
    tab_ref, halo_ref, taps_ref, first_ref,
    norm_ref, slope_ref, q_ref, x_ref, sd_ref,
    slots_a, slots_b, buf, inbox, ex, ex_in, ex_out, erow,
    send_sems, recv_sems, stat_send, stat_recv, halo_sems,
):
    me = lax.axis_index("seq")
    rows = sd_ref.shape[0]
    channels = conv_ref.shape[1]
    utts = lengths_ref.shape[1]
    bits = n.bit_length() - 1
    low = min(3, bits)
    group = 1 << low
    groups = n // group
    my_low, my_high = me % group, me // group
    first_sample = me * (rows * TAPS)

    barrier = pltpu.get_barrier_semaphore()
    orders = stage_orders(bits)

    def flip(mask):
        out = me
        for b in range(bits):
            if mask >> b & 1:
                out = out + (1 - 2 * ((me // (1 << b)) % 2)) * (1 << b)
        return out

    stat_masks = list(range(1, group)) + [k * group for k in range(1, groups)]
    all_masks = sorted(set(stat_masks) | {1 << b for b in range(bits)})
    for mask in all_masks:
        pl.semaphore_signal(
            barrier, inc=1, device_id={"seq": flip(mask)}, device_id_type=MESH
        )
    pl.semaphore_signal(
        barrier, inc=1, device_id={"seq": lax.rem(me + 1, n)}, device_id_type=MESH
    )
    tab_ref[...] = jnp.zeros_like(tab_ref)
    tab_ref[0:rows, 0:TAPS] = wave_ref[...]
    first_ref[...] = jnp.zeros_like(first_ref)
    for t in range(3):
        first_ref[t * 128 + 5 * t : t * 128 + 5 * t + TAPS] = conv_ref[...]
    pl.semaphore_wait(barrier, len(all_masks) + 1)
    halo = pltpu.make_async_remote_copy(
        src_ref=tab_ref.at[pl.ds(0, 8)],
        dst_ref=halo_ref,
        send_sem=halo_sems.at[0],
        recv_sem=halo_sems.at[1],
        device_id={"seq": lax.rem(me + n - 1, n)},
        device_id_type=MESH,
    )
    halo.start()

    units = [lengths_ref[0, u] + (MIN_UNITS - 1) for u in range(utts)]
    ends, total = [], jnp.int32(0)
    for u in range(utts):
        total = total + units[u] * 640
        ends.append(total)
    here = jnp.int32(0)
    for u in range(utts - 1):
        here = here + jnp.where(first_sample >= ends[u], 1, 0)
    end_a, end_b = jnp.int32(0), jnp.int32(0)
    for u in range(utts):
        end_a = jnp.where(here == u, ends[u], end_a)
        end_b = jnp.where(here + 1 == u, ends[u], end_b)

    def masks(t, start, count, width):
        row = lax.broadcasted_iota(jnp.int32, (count, width), 0) + start
        place = first_sample + 5 * t + TAPS * row
        is_b = place >= end_a
        valid = place + TAPS <= jnp.where(is_b, end_b, end_a)
        return is_b, valid

    lane = lax.broadcasted_iota(jnp.int32, (BLOCK, 128), 1)
    lane_b = ((lane >= 32) & (lane < 64)) | (lane == 65)

    zero_row = jnp.zeros((1, channels), F32)
    sq = (zero_row, zero_row)
    for t in range(3):
        if t == 1:
            halo.wait_recv()
            tab_ref[rows : rows + 8] = jnp.where(me == n - 1, 0.0, halo_ref[...])
            own = tab_ref[0:rows] + pltpu.roll(tab_ref[1 : rows + 1], TAPS, 1)
            wide = lax.broadcasted_iota(jnp.int32, (rows, 128), 1)
            ones = jnp.where((wide == 64) | (wide == 65), 1.0, 0.0)
            taps_ref[...] = own + pltpu.roll(own, 32, 1) + ones

        def conv_block(i, carry, t=t):
            start = pl.multiple_of(i * BLOCK, BLOCK)
            at = pl.ds(pl.multiple_of(t * rows + i * BLOCK, BLOCK), BLOCK)
            taps = (taps_ref if t else tab_ref)[pl.ds(start, BLOCK)]
            weight = first_ref[t * 128 : (t + 1) * 128]
            pre = jnp.dot(taps, weight, precision=HIGH, preferred_element_type=F32)
            norm_ref[at] = pre
            if t == 2:
                return carry
            is_b, valid = masks(t, start, BLOCK, channels)
            square = jnp.where(valid, pre * pre, 0.0)
            in_b = jnp.where(is_b, square, 0.0)
            in_a = jnp.where(is_b, 0.0, square)
            return (
                carry[0] + jnp.sum(in_a, axis=0, keepdims=True),
                carry[1] + jnp.sum(in_b, axis=0, keepdims=True),
            )

        sq = lax.fori_loop(0, rows // BLOCK, conv_block, sq)

    def taps_block(i, carry):
        start = pl.multiple_of(i * BLOCK, BLOCK)
        taps = taps_ref[pl.ds(start, BLOCK)]
        for t in range(3):
            is_b, valid = masks(t, start, BLOCK, 128)
            at = pl.ds(pl.multiple_of(t * rows + i * BLOCK, BLOCK), BLOCK)
            q_ref[at] = jnp.where(valid & (is_b == lane_b), taps, 0.0)
        return carry

    lax.fori_loop(0, rows // BLOCK, taps_block, 0)

    def by_tap(ref, t):
        return dot_tn(q_ref[t * rows : (t + 1) * rows], ref[t * rows : (t + 1) * rows], HIGH)

    sums = [by_tap(norm_ref, t) for t in range(2)]
    pre_a = sums[0][0:TAPS] + sums[1][5 : 5 + TAPS]
    pre_b = sums[0][32 : 32 + TAPS] + sums[1][37 : 37 + TAPS]
    one_ab = sums[0][64:72] + sums[1][64:72]

    def spread(a, b):
        return [
            jnp.where(here == u, a, jnp.where(here + 1 == u, b, jnp.zeros_like(a)))
            for u in range(utts)
        ]

    stats = spread(one_ab[0:1], one_ab[1:2]) + spread(sq[0], sq[1])
    slots_a[my_low] = jnp.concatenate(stats, axis=0)

    def exchange(slots, mine, members, number):
        copies = []
        for i, mask in enumerate(members):
            copy = pltpu.make_async_remote_copy(
                src_ref=slots.at[mine],
                dst_ref=slots.at[mine],
                send_sem=stat_send.at[number + i],
                recv_sem=stat_recv.at[number + i],
                device_id={"seq": flip(mask)},
                device_id_type=MESH,
            )
            copy.start()
            copies.append(copy)
        return copies

    stat_copies = exchange(slots_a, my_low, range(group - 1, 0, -1), 0)
    qq = [by_tap(q_ref, t) for t in range(2)]
    w_rows = qq[0][64:72] + pltpu.roll(qq[1][64:72], 123, 1)
    w_a = qq[0][0:TAPS, 64:65] + qq[1][5 : 5 + TAPS, 64:65]
    w_b = qq[0][32 : 32 + TAPS, 65:66] + qq[1][37 : 37 + TAPS, 65:66]
    for copy in stat_copies:
        copy.wait_recv()
    total = slots_a[0]
    for i in range(1, group):
        total = total + slots_a[i]
    if groups > 1:
        slots_b[my_high] = total
        more = exchange(slots_b, my_high, [k * group for k in range(groups - 1, 0, -1)], group - 1)
        for copy in more:
            copy.wait_recv()
        stat_copies = stat_copies + more
        total = slots_b[0]
        for i in range(1, groups):
            total = total + slots_b[i]
    means, rstds, counts = [], [], []
    for u in range(utts):
        count = jnp.full((1, channels), units[u] * 128 - 1, jnp.int32).astype(F32)
        mean = total[u : u + 1] / count
        var = total[utts + u : utts + u + 1] / count - mean * mean
        means.append(mean)
        rstds.append(lax.rsqrt(var + 1e-05))
        counts.append(count)

    def pick(values, offset):
        out = zero_row
        for u in range(utts):
            out = jnp.where(here + offset == u, values[u], out)
        return out

    mean_a, mean_b = pick(means, 0), pick(means, 1)
    rstd_a, rstd_b = pick(rstds, 0), pick(rstds, 1)

    for t in range(3):
        def gelu_block(i, carry, t=t):
            start = pl.multiple_of(i * 32, 32)
            at = pl.ds(pl.multiple_of(t * rows + i * 32, 32), 32)
            is_b, valid = masks(t, start, 32, channels)
            norm = (norm_ref[at] - jnp.where(is_b, mean_b, mean_a)) * jnp.where(
                is_b, rstd_b, rstd_a
            )
            norm_ref[at] = norm
            cdf = 0.5 * (1.0 + lax.erf(norm * 0.7071067811865476))
            x_ref[at] = jnp.where(valid, norm * cdf, 0.0).astype(jnp.bfloat16)
            slope = cdf + norm * jnp.exp(-0.5 * norm * norm) * 0.3989422804014327
            slope_ref[at] = jnp.where(valid, slope, 0.0)
            return carry

        lax.fori_loop(0, rows // 32, gelu_block, 0)

    def second_block(i, carry):
        start = pl.multiple_of(i * 128, 128)
        pre = jnp.zeros((128, channels), F32)
        for t in range(3):
            pre = pre + jnp.dot(
                x_ref[pl.ds(pl.multiple_of(t * rows + i * 128, 128), 128)],
                second_ref[t * channels : (t + 1) * channels],
                preferred_element_type=F32,
            )
        row = lax.broadcasted_iota(jnp.int32, (128, channels), 0) + start
        place = first_sample + TAPS * row
        valid = place + 2 * TAPS <= jnp.where(place >= end_a, end_b, end_a)
        cdf = 0.5 * (1.0 + lax.erf(pre * 0.7071067811865476))
        at = pl.ds(start, 128)
        feat_ref[at] = jnp.where(valid, pre * cdf, 0.0).astype(jnp.bfloat16)
        slope = cdf + pre * jnp.exp(-0.5 * pre * pre) * 0.3989422804014327
        sd_ref[at] = jnp.where(valid, cot_ref[at].astype(F32) * slope, 0.0).astype(jnp.bfloat16)
        return carry

    lax.fori_loop(0, rows // 128, second_block, 0)

    blocks = channels // 128
    tall = channels // 8
    size = blocks * tall
    parts = []
    for t in range(3):
        part = Part(
            me, orders[t], buf.at[pl.ds(t * size, size)], inbox.at[pl.ds(t * size, size)],
            outb.at[pl.ds(t * size, size)], size, send_sems.at[t], recv_sems.at[t],
        )
        grad = dot_tn(x_ref[t * rows : (t + 1) * rows], sd_ref[...])
        for c in range(blocks):
            buf[t * size + c * tall : t * size + (c + 1) * tall] = grad[
                :, c * 128 : (c + 1) * 128
            ].reshape(tall, 8, 128)
        part.start()
        parts.append(part)

    back = (zero_row, zero_row, zero_row, zero_row)
    for t in range(3):
        here_t = pl.ds(t * rows, rows)
        slope_ref[here_t] = slope_ref[here_t] * dot_nt(
            sd_ref[...], second_ref[t * channels : (t + 1) * channels]
        )

        def back_block(i, carry, t=t):
            start = pl.multiple_of(i * BLOCK, BLOCK)
            at = pl.ds(pl.multiple_of(t * rows + i * BLOCK, BLOCK), BLOCK)
            delta = slope_ref[at]
            is_b, _ = masks(t, start, BLOCK, channels)
            scaled = delta * norm_ref[at]
            add = [jnp.where(is_b, 0.0, delta), jnp.where(is_b, delta, 0.0)]
            add += [jnp.where(is_b, 0.0, scaled), jnp.where(is_b, scaled, 0.0)]
            return tuple(c + jnp.sum(a, axis=0, keepdims=True) for c, a in zip(carry, add))

        back = lax.fori_loop(0, rows // BLOCK, back_block, back)
        for part in parts:
            part.step()
    acc = [by_tap(slope_ref, t) for t in range(3)]

    grad_a = jnp.zeros((TAPS, channels), F32)
    for t in range(3):
        grad_a = grad_a + rstd_a * acc[t][5 * t : 5 * t + TAPS]
        grad_a = grad_a + rstd_b * acc[t][32 + 5 * t : 32 + 5 * t + TAPS]
    erow[0:TAPS] = grad_a
    one = spread(back[0], back[1])
    two = spread(back[2], back[3])
    erow[16:24] = jnp.concatenate(one + two, axis=0)
    norm_a = rstd_a * (pre_a - w_a * mean_a)
    norm_b = rstd_b * (pre_b - w_b * mean_b)
    for u, value in enumerate(spread(norm_a, norm_b)):
        erow[24 + u * TAPS : 24 + (u + 1) * TAPS] = value
    erow[10:16] = jnp.zeros((6, channels), F32)
    for u, w in enumerate(spread(w_rows[0:1], w_rows[1:2])):
        erow[10 + u : 11 + u, 0:128] = w
    high = erow.shape[0] // 8
    for c in range(blocks):
        ex[c * high : (c + 1) * high] = erow[:, c * 128 : (c + 1) * 128].reshape(high, 8, 128)
    extra = Part(
        me, orders[3], ex, ex_in, ex_out, blocks * high, send_sems.at[3], recv_sems.at[3]
    )
    extra.start()
    for _ in range(2 * bits):
        for part in parts:
            if part.at < 2 * bits:
                part.step()
        extra.step()
    for c in range(blocks):
        erow[:, c * 128 : (c + 1) * 128] = ex_out[c * high : (c + 1) * high].reshape(8 * high, 128)
    weights, scales = [], []
    result = erow[0:TAPS]
    for u in range(utts):
        weights.append(erow[10 + u : 11 + u, 0:128])
        scales.append(rstds[u] * (erow[16 + u : 17 + u] / counts[u]))
        result = result - rstds[u] * (erow[16 + utts + u : 17 + utts + u] / counts[u]) * (
            erow[24 + u * TAPS : 24 + (u + 1) * TAPS]
        )
    pad = [jnp.zeros((8 - utts, 128), F32)], [jnp.zeros((8 - utts, channels), F32)]
    plain = dot_tn(
        jnp.concatenate(weights + pad[0], axis=0), jnp.concatenate(scales + pad[1], axis=0), HIGH
    )
    grad1_ref[...] = (result - plain[0:TAPS] - plain[32 : 32 + TAPS]) * factor
    halo.wait_send()
    for copy in stat_copies:
        copy.wait_send()
    for part in parts + [extra]:
        part.drain()


def finish(factor, feat_in, grad1_in, tiled_ref, feat_ref, grad1_ref, grad2_ref):
    feat_ref[...] = feat_in[...]
    grad1_ref[...] = grad1_in[...]
    grad2_ref[...] = tiled_ref[...].reshape(grad2_ref.shape) * factor


def on_device(waveform, lengths, conv_first, conv_second, cotangent):
    n = lax.axis_size("seq")
    samples = waveform[0]
    rows = samples.shape[0] // TAPS
    channels = conv_second.shape[1]
    utts = lengths.shape[1]
    assert 24 + utts * TAPS <= 64 and utts == 4 and samples.shape[0] < MIN_UNITS * 640
    count = 3 * rows
    factor = float(lax.axis_size("dp") * rows * n) ** (-0.5)
    tiles = 3 * channels // 8 * (channels // 128)
    small = 64 // 8 * (channels // 128)
    bits = n.bit_length() - 1
    vmem = pl.BlockSpec(memory_space=pltpu.VMEM)
    feats, grad1, tiled = pl.pallas_call(
        functools.partial(kernel, n, factor),
        name="encoder",
        out_shape=(
            jax.ShapeDtypeStruct((rows, channels), jnp.bfloat16),
            jax.ShapeDtypeStruct((TAPS, channels), F32),
            jax.ShapeDtypeStruct((tiles, 8, 128), F32),
        ),
        in_specs=[pl.BlockSpec(memory_space=pltpu.SMEM)] + [vmem] * 4,
        out_specs=(vmem, vmem, vmem),
        scratch_shapes=[
            pltpu.VMEM((rows + 8, 128), F32),
            pltpu.VMEM((8, 128), F32),
            pltpu.VMEM((rows, 128), F32),
            pltpu.VMEM((3 * 128, channels), F32),
            pltpu.VMEM((count, channels), F32),
            pltpu.VMEM((count, channels), F32),
            pltpu.VMEM((count, 128), F32),
            pltpu.VMEM((count, channels), jnp.bfloat16),
            pltpu.VMEM((rows, channels), jnp.bfloat16),
            pltpu.VMEM((8, 2 * utts, channels), F32),
            pltpu.VMEM((max(1, n // 8), 2 * utts, channels), F32),
            pltpu.VMEM((tiles, 8, 128), F32),
            pltpu.VMEM((tiles, 8, 128), F32),
            pltpu.VMEM((small, 8, 128), F32),
            pltpu.VMEM((small, 8, 128), F32),
            pltpu.VMEM((small, 8, 128), F32),
            pltpu.VMEM((64, channels), F32),
            pltpu.SemaphoreType.DMA((4, 2 * bits)),
            pltpu.SemaphoreType.DMA((4, 2 * bits)),
            pltpu.SemaphoreType.DMA((8 + n // 8,)),
            pltpu.SemaphoreType.DMA((8 + n // 8,)),
            pltpu.SemaphoreType.DMA((2,)),
        ],
        compiler_params=pltpu.CompilerParams(
            collective_id=0, has_side_effects=True, vmem_limit_bytes=60 * 1024 * 1024
        ),
    )(lengths, waveform.reshape(rows, TAPS), conv_first, conv_second, cotangent[0])
    cols = channels // 128
    feats, grad1, grad2 = pl.pallas_call(
        functools.partial(finish, factor),
        name="finish",
        grid=(cols,),
        out_shape=(
            jax.ShapeDtypeStruct((rows, channels), jnp.bfloat16),
            jax.ShapeDtypeStruct((TAPS, channels), F32),
            jax.ShapeDtypeStruct((3 * channels, channels), F32),
        ),
        in_specs=[
            pl.BlockSpec((rows // cols, channels), lambda i: (i, 0)),
            pl.BlockSpec((TAPS, 128), lambda i: (0, i)),
            pl.BlockSpec((3, 1, channels // 8, 8, 128), lambda i: (0, i, 0, 0, 0)),
        ],
        out_specs=(
            pl.BlockSpec((rows // cols, channels), lambda i: (i, 0)),
            pl.BlockSpec((TAPS, 128), lambda i: (0, i)),
            pl.BlockSpec((3 * channels, 128), lambda i: (0, i)),
        ),
    )(feats, grad1, tiled.reshape(3, cols, channels // 8, 8, 128))
    if lax.axis_size("dp") > 1:
        grad1, grad2 = lax.psum((grad1, grad2), "dp")
    return (feats[None], grad1, grad2)


def solution(mesh):
    placed = (P("dp", "seq"), P("dp", None), P(), P(), P("dp", "seq", None))
    return jax.shard_map(
        on_device,
        mesh=mesh,
        in_specs=placed,
        out_specs=(P("dp", "seq", None), P(), P()),
        check_vma=False,
    )
```

```python
import functools

import jax
import jax.numpy as jnp
from jax import lax
from jax.experimental import pallas as pl
from jax.experimental.pallas import tpu as pltpu
from jax.sharding import PartitionSpec as P

MIN_UNITS = 50
TAPS = 10
HIGH = lax.Precision.HIGHEST
MESH = pl.DeviceIdType.MESH
F32 = jnp.float32
BLOCK = 64


def dot_tn(a, b, precision=None):
    return lax.dot_general(
        a, b, (((0,), (0,)), ((), ())), precision=precision, preferred_element_type=F32
    )


def dot_nt(a, b):
    return lax.dot_general(a, b, (((1,), (1,)), ((), ())), preferred_element_type=F32)


def stage_orders(bits):
    if bits != 5:
        return [list(range(bits))] * 7
    return [
        [0, 1, 2, 3, 4], [0, 1, 3, 2, 4],
        [0, 2, 3, 1, 4], [0, 2, 1, 3, 4],
        [0, 3, 1, 2, 4], [0, 3, 2, 1, 4],
        [0, 1, 2, 3, 4],
    ]


class Part:
    def __init__(self, me, order, src, inbox, out, size, send_sems, recv_sems):
        self.me, self.order, self.src, self.inbox, self.out = me, order, src, inbox, out
        self.send_sems, self.recv_sems = send_sems, recv_sems
        self.stages = len(order)
        self.size, self.off, self.room, self.at = size, 0, 0, 0
        self.copies = []

    def bit(self, stage):
        return (self.me // (1 << self.order[stage])) % 2

    def send(self, src, dst, stage, number):
        partner = self.me + (1 - 2 * self.bit(stage)) * (1 << self.order[stage])
        copy = pltpu.make_async_remote_copy(
            src_ref=src,
            dst_ref=dst,
            send_sem=self.send_sems.at[number],
            recv_sem=self.recv_sems.at[number],
            device_id={"seq": partner},
            device_id_type=MESH,
        )
        copy.start()
        self.copies.append(copy)

    def start(self):
        if self.at < self.stages:
            half = self.size // 2
            bit = self.bit(self.at)
            self.send(
                self.src.at[pl.ds(self.off + (1 - bit) * half, half)],
                self.inbox.at[pl.ds(self.room, half)],
                self.at,
                self.at,
            )
            self.off = self.off + bit * half
            self.size = half
        elif self.at < 2 * self.stages:
            own = self.out.at[pl.ds(self.off, self.size)]
            self.send(own, own, 2 * self.stages - 1 - self.at, self.at)

    def finish(self):
        self.copies[self.at].wait_recv()
        if self.at < self.stages:
            last = self.at == self.stages - 1
            target = self.out if last else self.src
            step = min(self.size, 16)

            def add(i, carry):
                here = pl.ds(self.off + i * step, step)
                target[here] = self.src[here] + self.inbox[pl.ds(self.room + i * step, step)]
                return carry

            lax.fori_loop(0, self.size // step, add, 0)
            self.room += self.size
        else:
            bit = self.bit(2 * self.stages - 1 - self.at)
            self.off = self.off - bit * self.size
            self.size = self.size * 2
        self.at += 1

    def step(self):
        self.finish()
        self.start()

    def drain(self):
        for copy in self.copies:
            copy.wait_send()


def kernel(
    n, factor,
    lengths_ref, wave_ref, conv_ref, second_ref, cot_ref,
    feat_ref, grad1_ref, outb,
    tab_ref, halo_ref, taps_ref, first_ref,
    norm_ref, slope_ref, q_ref, x_ref, sd_ref,
    slots_a, slots_b, buf, inbox, ex, ex_in, ex_out, erow,
    send_sems, recv_sems, stat_send, stat_recv, halo_sems,
):
    me = lax.axis_index("seq")
    rows = sd_ref.shape[0]
    channels = conv_ref.shape[1]
    utts = lengths_ref.shape[1]
    bits = n.bit_length() - 1
    low = min(3, bits)
    group = 1 << low
    groups = n // group
    my_low, my_high = me % group, me // group
    first_sample = me * (rows * TAPS)

    barrier = pltpu.get_barrier_semaphore()
    orders = stage_orders(bits)

    def flip(mask):
        out = me
        for b in range(bits):
            if mask >> b & 1:
                out = out + (1 - 2 * ((me // (1 << b)) % 2)) * (1 << b)
        return out

    stat_masks = list(range(1, group)) + [k * group for k in range(1, groups)]
    all_masks = sorted(set(stat_masks) | {1 << b for b in range(bits)})
    for mask in all_masks:
        pl.semaphore_signal(
            barrier, inc=1, device_id={"seq": flip(mask)}, device_id_type=MESH
        )
    pl.semaphore_signal(
        barrier, inc=1, device_id={"seq": lax.rem(me + 1, n)}, device_id_type=MESH
    )
    tab_ref[...] = jnp.zeros_like(tab_ref)
    tab_ref[0:rows, 0:TAPS] = wave_ref[...]
    first_ref[...] = jnp.zeros_like(first_ref)
    for t in range(3):
        first_ref[t * 128 + 5 * t : t * 128 + 5 * t + TAPS] = conv_ref[...]
    pl.semaphore_wait(barrier, len(all_masks) + 1)
    halo = pltpu.make_async_remote_copy(
        src_ref=tab_ref.at[pl.ds(0, 8)],
        dst_ref=halo_ref,
        send_sem=halo_sems.at[0],
        recv_sem=halo_sems.at[1],
        device_id={"seq": lax.rem(me + n - 1, n)},
        device_id_type=MESH,
    )
    halo.start()

    units = [lengths_ref[0, u] + (MIN_UNITS - 1) for u in range(utts)]
    ends, total = [], jnp.int32(0)
    for u in range(utts):
        total = total + units[u] * 640
        ends.append(total)
    here = jnp.int32(0)
    for u in range(utts - 1):
        here = here + jnp.where(first_sample >= ends[u], 1, 0)
    end_a, end_b = jnp.int32(0), jnp.int32(0)
    for u in range(utts):
        end_a = jnp.where(here == u, ends[u], end_a)
        end_b = jnp.where(here + 1 == u, ends[u], end_b)

    def masks(t, start, count, width):
        row = lax.broadcasted_iota(jnp.int32, (count, width), 0) + start
        place = first_sample + 5 * t + TAPS * row
        is_b = place >= end_a
        valid = place + TAPS <= jnp.where(is_b, end_b, end_a)
        return is_b, valid

    lane = lax.broadcasted_iota(jnp.int32, (BLOCK, 128), 1)
    lane_b = ((lane >= 32) & (lane < 64)) | (lane == 65)

    zero_row = jnp.zeros((1, channels), F32)
    sq = (zero_row, zero_row)
    for t in range(3):
        if t == 1:
            halo.wait_recv()
            tab_ref[rows : rows + 8] = jnp.where(me == n - 1, 0.0, halo_ref[...])
            own = tab_ref[0:rows] + pltpu.roll(tab_ref[1 : rows + 1], TAPS, 1)
            wide = lax.broadcasted_iota(jnp.int32, (rows, 128), 1)
            ones = jnp.where((wide == 64) | (wide == 65), 1.0, 0.0)
            taps_ref[...] = own + pltpu.roll(own, 32, 1) + ones

        def conv_block(i, carry, t=t):
            start = pl.multiple_of(i * BLOCK, BLOCK)
            at = pl.ds(pl.multiple_of(t * rows + i * BLOCK, BLOCK), BLOCK)
            taps = (taps_ref if t else tab_ref)[pl.ds(start, BLOCK)]
            weight = first_ref[t * 128 : (t + 1) * 128]
            pre = jnp.dot(taps, weight, precision=HIGH, preferred_element_type=F32)
            norm_ref[at] = pre
            if t == 2:
                return carry
            is_b, valid = masks(t, start, BLOCK, channels)
            square = jnp.where(valid, pre * pre, 0.0)
            in_b = jnp.where(is_b, square, 0.0)
            in_a = jnp.where(is_b, 0.0, square)
            return (
                carry[0] + jnp.sum(in_a, axis=0, keepdims=True),
                carry[1] + jnp.sum(in_b, axis=0, keepdims=True),
            )

        sq = lax.fori_loop(0, rows // BLOCK, conv_block, sq)

    def taps_block(i, carry):
        start = pl.multiple_of(i * BLOCK, BLOCK)
        taps = taps_ref[pl.ds(start, BLOCK)]
        for t in range(3):
            is_b, valid = masks(t, start, BLOCK, 128)
            at = pl.ds(pl.multiple_of(t * rows + i * BLOCK, BLOCK), BLOCK)
            q_ref[at] = jnp.where(valid & (is_b == lane_b), taps, 0.0)
        return carry

    lax.fori_loop(0, rows // BLOCK, taps_block, 0)

    def by_tap(ref, t):
        return dot_tn(q_ref[t * rows : (t + 1) * rows], ref[t * rows : (t + 1) * rows], HIGH)

    sums = [by_tap(norm_ref, t) for t in range(2)]
    pre_a = sums[0][0:TAPS] + sums[1][5 : 5 + TAPS]
    pre_b = sums[0][32 : 32 + TAPS] + sums[1][37 : 37 + TAPS]
    one_ab = sums[0][64:72] + sums[1][64:72]

    def spread(a, b):
        return [
            jnp.where(here == u, a, jnp.where(here + 1 == u, b, jnp.zeros_like(a)))
            for u in range(utts)
        ]

    stats = spread(one_ab[0:1], one_ab[1:2]) + spread(sq[0], sq[1])
    slots_a[my_low] = jnp.concatenate(stats, axis=0)

    def exchange(slots, mine, members, number):
        copies = []
        for i, mask in enumerate(members):
            copy = pltpu.make_async_remote_copy(
                src_ref=slots.at[mine],
                dst_ref=slots.at[mine],
                send_sem=stat_send.at[number + i],
                recv_sem=stat_recv.at[number + i],
                device_id={"seq": flip(mask)},
                device_id_type=MESH,
            )
            copy.start()
            copies.append(copy)
        return copies

    stat_copies = exchange(slots_a, my_low, range(group - 1, 0, -1), 0)
    qq = [by_tap(q_ref, t) for t in range(2)]
    w_rows = qq[0][64:72] + pltpu.roll(qq[1][64:72], 123, 1)
    w_a = qq[0][0:TAPS, 64:65] + qq[1][5 : 5 + TAPS, 64:65]
    w_b = qq[0][32 : 32 + TAPS, 65:66] + qq[1][37 : 37 + TAPS, 65:66]
    for copy in stat_copies:
        copy.wait_recv()
    total = slots_a[0]
    for i in range(1, group):
        total = total + slots_a[i]
    if groups > 1:
        slots_b[my_high] = total
        more = exchange(slots_b, my_high, [k * group for k in range(groups - 1, 0, -1)], group - 1)
        for copy in more:
            copy.wait_recv()
        stat_copies = stat_copies + more
        total = slots_b[0]
        for i in range(1, groups):
            total = total + slots_b[i]
    means, rstds, counts = [], [], []
    for u in range(utts):
        count = jnp.full((1, channels), units[u] * 128 - 1, jnp.int32).astype(F32)
        mean = total[u : u + 1] / count
        var = total[utts + u : utts + u + 1] / count - mean * mean
        means.append(mean)
        rstds.append(lax.rsqrt(var + 1e-05))
        counts.append(count)

    def pick(values, offset):
        out = zero_row
        for u in range(utts):
            out = jnp.where(here + offset == u, values[u], out)
        return out

    mean_a, mean_b = pick(means, 0), pick(means, 1)
    rstd_a, rstd_b = pick(rstds, 0), pick(rstds, 1)

    for t in range(3):
        def gelu_block(i, carry, t=t):
            start = pl.multiple_of(i * 32, 32)
            at = pl.ds(pl.multiple_of(t * rows + i * 32, 32), 32)
            is_b, valid = masks(t, start, 32, channels)
            norm = (norm_ref[at] - jnp.where(is_b, mean_b, mean_a)) * jnp.where(
                is_b, rstd_b, rstd_a
            )
            norm_ref[at] = norm
            cdf = 0.5 * (1.0 + lax.erf(norm * 0.7071067811865476))
            x_ref[at] = jnp.where(valid, norm * cdf, 0.0).astype(jnp.bfloat16)
            slope = cdf + norm * jnp.exp(-0.5 * norm * norm) * 0.3989422804014327
            slope_ref[at] = jnp.where(valid, slope, 0.0)
            return carry

        lax.fori_loop(0, rows // 32, gelu_block, 0)

    def second_block(i, carry):
        start = pl.multiple_of(i * 128, 128)
        pre = jnp.zeros((128, channels), F32)
        for t in range(3):
            pre = pre + jnp.dot(
                x_ref[pl.ds(pl.multiple_of(t * rows + i * 128, 128), 128)],
                second_ref[t * channels : (t + 1) * channels],
                preferred_element_type=F32,
            )
        row = lax.broadcasted_iota(jnp.int32, (128, channels), 0) + start
        place = first_sample + TAPS * row
        valid = place + 2 * TAPS <= jnp.where(place >= end_a, end_b, end_a)
        cdf = 0.5 * (1.0 + lax.erf(pre * 0.7071067811865476))
        at = pl.ds(start, 128)
        feat_ref[at] = jnp.where(valid, pre * cdf, 0.0).astype(jnp.bfloat16)
        slope = cdf + pre * jnp.exp(-0.5 * pre * pre) * 0.3989422804014327
        sd_ref[at] = jnp.where(valid, cot_ref[at].astype(F32) * slope, 0.0).astype(jnp.bfloat16)
        return carry

    lax.fori_loop(0, rows // 128, second_block, 0)

    blocks = channels // 128
    tall = channels // 8
    size = blocks * tall
    parts = []
    for t in range(3):
        grad = dot_tn(x_ref[t * rows : (t + 1) * rows], sd_ref[...])
        for c in range(blocks):
            buf[t * size + c * tall : t * size + (c + 1) * tall] = grad[
                :, c * 128 : (c + 1) * 128
            ].reshape(tall, 8, 128)
        for k in (2 * t, 2 * t + 1):
            at = pl.ds(k * (size // 2), size // 2)
            part = Part(
                me, orders[k], buf.at[at], inbox.at[at], outb.at[at], size // 2,
                send_sems.at[k], recv_sems.at[k],
            )
            part.start()
            parts.append(part)

    back = (zero_row, zero_row, zero_row, zero_row)
    for t in range(3):
        here_t = pl.ds(t * rows, rows)
        slope_ref[here_t] = slope_ref[here_t] * dot_nt(
            sd_ref[...], second_ref[t * channels : (t + 1) * channels]
        )

        def back_block(i, carry, t=t):
            start = pl.multiple_of(i * BLOCK, BLOCK)
            at = pl.ds(pl.multiple_of(t * rows + i * BLOCK, BLOCK), BLOCK)
            delta = slope_ref[at]
            is_b, _ = masks(t, start, BLOCK, channels)
            scaled = delta * norm_ref[at]
            add = [jnp.where(is_b, 0.0, delta), jnp.where(is_b, delta, 0.0)]
            add += [jnp.where(is_b, 0.0, scaled), jnp.where(is_b, scaled, 0.0)]
            return tuple(c + jnp.sum(a, axis=0, keepdims=True) for c, a in zip(carry, add))

        back = lax.fori_loop(0, rows // BLOCK, back_block, back)
        for part in parts:
            part.step()
    acc = [by_tap(slope_ref, t) for t in range(3)]

    grad_a = jnp.zeros((TAPS, channels), F32)
    for t in range(3):
        grad_a = grad_a + rstd_a * acc[t][5 * t : 5 * t + TAPS]
        grad_a = grad_a + rstd_b * acc[t][32 + 5 * t : 32 + 5 * t + TAPS]
    erow[0:TAPS] = grad_a
    one = spread(back[0], back[1])
    two = spread(back[2], back[3])
    erow[16:24] = jnp.concatenate(one + two, axis=0)
    norm_a = rstd_a * (pre_a - w_a * mean_a)
    norm_b = rstd_b * (pre_b - w_b * mean_b)
    for u, value in enumerate(spread(norm_a, norm_b)):
        erow[24 + u * TAPS : 24 + (u + 1) * TAPS] = value
    erow[10:16] = jnp.zeros((6, channels), F32)
    for u, w in enumerate(spread(w_rows[0:1], w_rows[1:2])):
        erow[10 + u : 11 + u, 0:128] = w
    high = erow.shape[0] // 8
    for c in range(blocks):
        ex[c * high : (c + 1) * high] = erow[:, c * 128 : (c + 1) * 128].reshape(high, 8, 128)
    extra = Part(
        me, orders[6], ex, ex_in, ex_out, blocks * high, send_sems.at[6], recv_sems.at[6]
    )
    extra.start()
    for _ in range(2 * bits):
        for part in parts:
            if part.at < 2 * bits:
                part.step()
        extra.step()
    for c in range(blocks):
        erow[:, c * 128 : (c + 1) * 128] = ex_out[c * high : (c + 1) * high].reshape(8 * high, 128)
    weights, scales = [], []
    result = erow[0:TAPS]
    for u in range(utts):
        weights.append(erow[10 + u : 11 + u, 0:128])
        scales.append(rstds[u] * (erow[16 + u : 17 + u] / counts[u]))
        result = result - rstds[u] * (erow[16 + utts + u : 17 + utts + u] / counts[u]) * (
            erow[24 + u * TAPS : 24 + (u + 1) * TAPS]
        )
    pad = [jnp.zeros((8 - utts, 128), F32)], [jnp.zeros((8 - utts, channels), F32)]
    plain = dot_tn(
        jnp.concatenate(weights + pad[0], axis=0), jnp.concatenate(scales + pad[1], axis=0), HIGH
    )
    grad1_ref[...] = (result - plain[0:TAPS] - plain[32 : 32 + TAPS]) * factor
    halo.wait_send()
    for copy in stat_copies:
        copy.wait_send()
    for part in parts + [extra]:
        part.drain()


def finish(factor, feat_in, grad1_in, tiled_ref, feat_ref, grad1_ref, grad2_ref):
    feat_ref[...] = feat_in[...]
    grad1_ref[...] = grad1_in[...]
    grad2_ref[...] = tiled_ref[...].reshape(grad2_ref.shape) * factor


def on_device(waveform, lengths, conv_first, conv_second, cotangent):
    n = lax.axis_size("seq")
    samples = waveform[0]
    rows = samples.shape[0] // TAPS
    channels = conv_second.shape[1]
    utts = lengths.shape[1]
    assert 24 + utts * TAPS <= 64 and utts == 4 and samples.shape[0] < MIN_UNITS * 640
    count = 3 * rows
    factor = float(lax.axis_size("dp") * rows * n) ** (-0.5)
    tiles = 3 * channels // 8 * (channels // 128)
    small = 64 // 8 * (channels // 128)
    bits = n.bit_length() - 1
    vmem = pl.BlockSpec(memory_space=pltpu.VMEM)
    feats, grad1, tiled = pl.pallas_call(
        functools.partial(kernel, n, factor),
        name="encoder",
        out_shape=(
            jax.ShapeDtypeStruct((rows, channels), jnp.bfloat16),
            jax.ShapeDtypeStruct((TAPS, channels), F32),
            jax.ShapeDtypeStruct((tiles, 8, 128), F32),
        ),
        in_specs=[pl.BlockSpec(memory_space=pltpu.SMEM)] + [vmem] * 4,
        out_specs=(vmem, vmem, vmem),
        scratch_shapes=[
            pltpu.VMEM((rows + 8, 128), F32),
            pltpu.VMEM((8, 128), F32),
            pltpu.VMEM((rows, 128), F32),
            pltpu.VMEM((3 * 128, channels), F32),
            pltpu.VMEM((count, channels), F32),
            pltpu.VMEM((count, channels), F32),
            pltpu.VMEM((count, 128), F32),
            pltpu.VMEM((count, channels), jnp.bfloat16),
            pltpu.VMEM((rows, channels), jnp.bfloat16),
            pltpu.VMEM((8, 2 * utts, channels), F32),
            pltpu.VMEM((max(1, n // 8), 2 * utts, channels), F32),
            pltpu.VMEM((tiles, 8, 128), F32),
            pltpu.VMEM((tiles, 8, 128), F32),
            pltpu.VMEM((small, 8, 128), F32),
            pltpu.VMEM((small, 8, 128), F32),
            pltpu.VMEM((small, 8, 128), F32),
            pltpu.VMEM((64, channels), F32),
            pltpu.SemaphoreType.DMA((7, 2 * bits)),
            pltpu.SemaphoreType.DMA((7, 2 * bits)),
            pltpu.SemaphoreType.DMA((8 + n // 8,)),
            pltpu.SemaphoreType.DMA((8 + n // 8,)),
            pltpu.SemaphoreType.DMA((2,)),
        ],
        compiler_params=pltpu.CompilerParams(
            collective_id=0, has_side_effects=True, vmem_limit_bytes=60 * 1024 * 1024
        ),
    )(lengths, waveform.reshape(rows, TAPS), conv_first, conv_second, cotangent[0])
    cols = channels // 128
    feats, grad1, grad2 = pl.pallas_call(
        functools.partial(finish, factor),
        name="finish",
        grid=(cols,),
        out_shape=(
            jax.ShapeDtypeStruct((rows, channels), jnp.bfloat16),
            jax.ShapeDtypeStruct((TAPS, channels), F32),
            jax.ShapeDtypeStruct((3 * channels, channels), F32),
        ),
        in_specs=[
            pl.BlockSpec((rows // cols, channels), lambda i: (i, 0)),
            pl.BlockSpec((TAPS, 128), lambda i: (0, i)),
            pl.BlockSpec((3, 1, channels // 8, 8, 128), lambda i: (0, i, 0, 0, 0)),
        ],
        out_specs=(
            pl.BlockSpec((rows // cols, channels), lambda i: (i, 0)),
            pl.BlockSpec((TAPS, 128), lambda i: (0, i)),
            pl.BlockSpec((3 * channels, 128), lambda i: (0, i)),
        ),
    )(feats, grad1, tiled.reshape(3, cols, channels // 8, 8, 128))
    if lax.axis_size("dp") > 1:
        grad1, grad2 = lax.psum((grad1, grad2), "dp")
    return (feats[None], grad1, grad2)


def solution(mesh):
    placed = (P("dp", "seq"), P("dp", None), P(), P(), P("dp", "seq", None))
    return jax.shard_map(
        on_device,
        mesh=mesh,
        in_specs=placed,
        out_specs=(P("dp", "seq", None), P(), P()),
        check_vma=False,
    )
```

```python
import functools

import jax
import jax.numpy as jnp
from jax import lax
from jax.experimental import pallas as pl
from jax.experimental.pallas import tpu as pltpu
from jax.sharding import PartitionSpec as P

MIN_UNITS = 50
TAPS = 10
HIGH = lax.Precision.HIGHEST
MESH = pl.DeviceIdType.MESH
F32 = jnp.float32
BLOCK = 64


def dot_tn(a, b, precision=None):
    return lax.dot_general(
        a, b, (((0,), (0,)), ((), ())), precision=precision, preferred_element_type=F32
    )


def dot_nt(a, b):
    return lax.dot_general(a, b, (((1,), (1,)), ((), ())), preferred_element_type=F32)


def stage_orders(bits):
    if bits != 5:
        return [list(range(bits))] * 7
    return [
        [0, 1, 2, 3, 4], [0, 1, 3, 2, 4],
        [0, 2, 3, 1, 4], [0, 2, 1, 3, 4],
        [0, 3, 1, 2, 4], [0, 3, 2, 1, 4],
        [0, 1, 2, 3, 4],
    ]


class Part:
    def __init__(self, me, order, src, inbox, out, size, send_sems, recv_sems):
        self.me, self.order, self.src, self.inbox, self.out = me, order, src, inbox, out
        self.send_sems, self.recv_sems = send_sems, recv_sems
        self.stages = len(order)
        self.size, self.off, self.room, self.at = size, 0, 0, 0
        self.copies = []

    def bit(self, stage):
        return (self.me // (1 << self.order[stage])) % 2

    def send(self, src, dst, stage, number):
        partner = self.me + (1 - 2 * self.bit(stage)) * (1 << self.order[stage])
        copy = pltpu.make_async_remote_copy(
            src_ref=src,
            dst_ref=dst,
            send_sem=self.send_sems.at[number],
            recv_sem=self.recv_sems.at[number],
            device_id={"seq": partner},
            device_id_type=MESH,
        )
        copy.start()
        self.copies.append(copy)

    def start(self):
        if self.at < self.stages:
            half = self.size // 2
            bit = self.bit(self.at)
            self.send(
                self.src.at[pl.ds(self.off + (1 - bit) * half, half)],
                self.inbox.at[pl.ds(self.room, half)],
                self.at,
                self.at,
            )
            self.off = self.off + bit * half
            self.size = half
        elif self.at < 2 * self.stages:
            own = self.out.at[pl.ds(self.off, self.size)]
            self.send(own, own, 2 * self.stages - 1 - self.at, self.at)

    def finish(self):
        self.copies[self.at].wait_recv()
        if self.at < self.stages:
            last = self.at == self.stages - 1
            target = self.out if last else self.src
            step = min(self.size, 16)

            def add(i, carry):
                here = pl.ds(self.off + i * step, step)
                target[here] = self.src[here] + self.inbox[pl.ds(self.room + i * step, step)]
                return carry

            lax.fori_loop(0, self.size // step, add, 0)
            self.room += self.size
        else:
            bit = self.bit(2 * self.stages - 1 - self.at)
            self.off = self.off - bit * self.size
            self.size = self.size * 2
        self.at += 1

    def step(self):
        self.finish()
        self.start()

    def drain(self):
        for copy in self.copies:
            copy.wait_send()


def kernel(
    n, factor,
    lengths_ref, wave_ref, conv_ref, second_ref, cot_ref,
    feat_ref, grad1_ref, outb,
    tab_ref, halo_ref, taps_ref, first_ref,
    norm_ref, slope_ref, q_ref, x_ref, sd_ref,
    slots_a, slots_b, buf, inbox, ex, ex_in, ex_out, erow,
    send_sems, recv_sems, stat_send, stat_recv, halo_sems,
):
    me = lax.axis_index("seq")
    rows = sd_ref.shape[0]
    channels = conv_ref.shape[1]
    utts = lengths_ref.shape[1]
    bits = n.bit_length() - 1
    low = min(3, bits)
    group = 1 << low
    groups = n // group
    my_low, my_high = me % group, me // group
    first_sample = me * (rows * TAPS)

    barrier = pltpu.get_barrier_semaphore()
    orders = stage_orders(bits)

    def flip(mask):
        out = me
        for b in range(bits):
            if mask >> b & 1:
                out = out + (1 - 2 * ((me // (1 << b)) % 2)) * (1 << b)
        return out

    stat_masks = list(range(1, group)) + [k * group for k in range(1, groups)]
    all_masks = sorted(set(stat_masks) | {1 << b for b in range(bits)})
    for mask in all_masks:
        pl.semaphore_signal(
            barrier, inc=1, device_id={"seq": flip(mask)}, device_id_type=MESH
        )
    pl.semaphore_signal(
        barrier, inc=1, device_id={"seq": lax.rem(me + 1, n)}, device_id_type=MESH
    )
    tab_ref[...] = jnp.zeros_like(tab_ref)
    tab_ref[0 : rows + 8, 0:TAPS] = wave_ref[...]
    first_ref[...] = jnp.zeros_like(first_ref)
    for t in range(3):
        first_ref[t * 128 + 5 * t : t * 128 + 5 * t + TAPS] = conv_ref[...]
    pl.semaphore_wait(barrier, len(all_masks) + 1)
    halo = pltpu.make_async_remote_copy(
        src_ref=tab_ref.at[pl.ds(0, 8)],
        dst_ref=halo_ref,
        send_sem=halo_sems.at[0],
        recv_sem=halo_sems.at[1],
        device_id={"seq": lax.rem(me + n - 1, n)},
        device_id_type=MESH,
    )
    halo.start()

    units = [lengths_ref[0, u] + (MIN_UNITS - 1) for u in range(utts)]
    ends, total = [], jnp.int32(0)
    for u in range(utts):
        total = total + units[u] * 640
        ends.append(total)
    here = jnp.int32(0)
    for u in range(utts - 1):
        here = here + jnp.where(first_sample >= ends[u], 1, 0)
    end_a, end_b = jnp.int32(0), jnp.int32(0)
    for u in range(utts):
        end_a = jnp.where(here == u, ends[u], end_a)
        end_b = jnp.where(here + 1 == u, ends[u], end_b)

    def masks(t, start, count, width):
        row = lax.broadcasted_iota(jnp.int32, (count, width), 0) + start
        place = first_sample + 5 * t + TAPS * row
        is_b = place >= end_a
        valid = place + TAPS <= jnp.where(is_b, end_b, end_a)
        return is_b, valid

    lane = lax.broadcasted_iota(jnp.int32, (BLOCK, 128), 1)
    lane_b = ((lane >= 32) & (lane < 64)) | (lane == 65)

    zero_row = jnp.zeros((1, channels), F32)
    sq = (zero_row, zero_row)
    for t in range(3):
        if t == 1:
            halo.wait_recv()
            tab_ref[rows : rows + 8] = jnp.where(me == n - 1, 0.0, halo_ref[...])
            own = tab_ref[0:rows] + pltpu.roll(tab_ref[1 : rows + 1], TAPS, 1)
            wide = lax.broadcasted_iota(jnp.int32, (rows, 128), 1)
            ones = jnp.where((wide == 64) | (wide == 65), 1.0, 0.0)
            taps_ref[...] = own + pltpu.roll(own, 32, 1) + ones

        def conv_block(i, carry, t=t):
            start = pl.multiple_of(i * BLOCK, BLOCK)
            at = pl.ds(pl.multiple_of(t * rows + i * BLOCK, BLOCK), BLOCK)
            taps = (taps_ref if t else tab_ref)[pl.ds(start, BLOCK)]
            weight = first_ref[t * 128 : (t + 1) * 128]
            pre = jnp.dot(taps, weight, precision=HIGH, preferred_element_type=F32)
            norm_ref[at] = pre
            if t == 2:
                return carry
            is_b, valid = masks(t, start, BLOCK, channels)
            square = jnp.where(valid, pre * pre, 0.0)
            in_b = jnp.where(is_b, square, 0.0)
            in_a = jnp.where(is_b, 0.0, square)
            return (
                carry[0] + jnp.sum(in_a, axis=0, keepdims=True),
                carry[1] + jnp.sum(in_b, axis=0, keepdims=True),
            )

        sq = lax.fori_loop(0, rows // BLOCK, conv_block, sq)

    def taps_block(i, carry):
        start = pl.multiple_of(i * BLOCK, BLOCK)
        taps = taps_ref[pl.ds(start, BLOCK)]
        for t in range(3):
            is_b, valid = masks(t, start, BLOCK, 128)
            at = pl.ds(pl.multiple_of(t * rows + i * BLOCK, BLOCK), BLOCK)
            q_ref[at] = jnp.where(valid & (is_b == lane_b), taps, 0.0)
        return carry

    lax.fori_loop(0, rows // BLOCK, taps_block, 0)

    def by_tap(ref, t):
        return dot_tn(q_ref[t * rows : (t + 1) * rows], ref[t * rows : (t + 1) * rows], HIGH)

    sums = [by_tap(norm_ref, t) for t in range(2)]
    pre_a = sums[0][0:TAPS] + sums[1][5 : 5 + TAPS]
    pre_b = sums[0][32 : 32 + TAPS] + sums[1][37 : 37 + TAPS]
    one_ab = sums[0][64:72] + sums[1][64:72]

    def spread(a, b):
        return [
            jnp.where(here == u, a, jnp.where(here + 1 == u, b, jnp.zeros_like(a)))
            for u in range(utts)
        ]

    stats = spread(one_ab[0:1], one_ab[1:2]) + spread(sq[0], sq[1])
    slots_a[my_low] = jnp.concatenate(stats, axis=0)

    def exchange(slots, mine, members, number):
        copies = []
        for i, mask in enumerate(members):
            copy = pltpu.make_async_remote_copy(
                src_ref=slots.at[mine],
                dst_ref=slots.at[mine],
                send_sem=stat_send.at[number + i],
                recv_sem=stat_recv.at[number + i],
                device_id={"seq": flip(mask)},
                device_id_type=MESH,
            )
            copy.start()
            copies.append(copy)
        return copies

    stat_copies = exchange(slots_a, my_low, range(group - 1, 0, -1), 0)
    qq = [by_tap(q_ref, t) for t in range(2)]
    w_rows = qq[0][64:72] + pltpu.roll(qq[1][64:72], 123, 1)
    w_a = qq[0][0:TAPS, 64:65] + qq[1][5 : 5 + TAPS, 64:65]
    w_b = qq[0][32 : 32 + TAPS, 65:66] + qq[1][37 : 37 + TAPS, 65:66]
    for copy in stat_copies:
        copy.wait_recv()
    total = slots_a[0]
    for i in range(1, group):
        total = total + slots_a[i]
    if groups > 1:
        slots_b[my_high] = total
        more = exchange(slots_b, my_high, [k * group for k in range(groups - 1, 0, -1)], group - 1)
        for copy in more:
            copy.wait_recv()
        stat_copies = stat_copies + more
        total = slots_b[0]
        for i in range(1, groups):
            total = total + slots_b[i]
    means, rstds, counts = [], [], []
    for u in range(utts):
        count = jnp.full((1, channels), units[u] * 128 - 1, jnp.int32).astype(F32)
        mean = total[u : u + 1] / count
        var = total[utts + u : utts + u + 1] / count - mean * mean
        means.append(mean)
        rstds.append(lax.rsqrt(var + 1e-05))
        counts.append(count)

    def pick(values, offset):
        out = zero_row
        for u in range(utts):
            out = jnp.where(here + offset == u, values[u], out)
        return out

    mean_a, mean_b = pick(means, 0), pick(means, 1)
    rstd_a, rstd_b = pick(rstds, 0), pick(rstds, 1)

    for t in range(3):
        def gelu_block(i, carry, t=t):
            start = pl.multiple_of(i * 32, 32)
            at = pl.ds(pl.multiple_of(t * rows + i * 32, 32), 32)
            is_b, valid = masks(t, start, 32, channels)
            norm = (norm_ref[at] - jnp.where(is_b, mean_b, mean_a)) * jnp.where(
                is_b, rstd_b, rstd_a
            )
            norm_ref[at] = norm
            cdf = 0.5 * (1.0 + lax.erf(norm * 0.7071067811865476))
            x_ref[at] = jnp.where(valid, norm * cdf, 0.0).astype(jnp.bfloat16)
            slope = cdf + norm * jnp.exp(-0.5 * norm * norm) * 0.3989422804014327
            slope_ref[at] = jnp.where(valid, slope, 0.0)
            return carry

        lax.fori_loop(0, rows // 32, gelu_block, 0)

    def second_block(i, carry):
        start = pl.multiple_of(i * 128, 128)
        pre = jnp.zeros((128, channels), F32)
        for t in range(3):
            pre = pre + jnp.dot(
                x_ref[pl.ds(pl.multiple_of(t * rows + i * 128, 128), 128)],
                second_ref[t * channels : (t + 1) * channels],
                preferred_element_type=F32,
            )
        row = lax.broadcasted_iota(jnp.int32, (128, channels), 0) + start
        place = first_sample + TAPS * row
        valid = place + 2 * TAPS <= jnp.where(place >= end_a, end_b, end_a)
        cdf = 0.5 * (1.0 + lax.erf(pre * 0.7071067811865476))
        at = pl.ds(start, 128)
        feat_ref[at] = jnp.where(valid, pre * cdf, 0.0).astype(jnp.bfloat16)
        slope = cdf + pre * jnp.exp(-0.5 * pre * pre) * 0.3989422804014327
        sd_ref[at] = jnp.where(valid, cot_ref[at].astype(F32) * slope, 0.0).astype(jnp.bfloat16)
        return carry

    lax.fori_loop(0, rows // 128, second_block, 0)

    blocks = channels // 128
    tall = channels // 8
    size = blocks * tall
    parts = []
    for t in range(3):
        grad = dot_tn(x_ref[t * rows : (t + 1) * rows], sd_ref[...])
        for c in range(blocks):
            buf[t * size + c * tall : t * size + (c + 1) * tall] = grad[
                :, c * 128 : (c + 1) * 128
            ].reshape(tall, 8, 128)
        for k in (2 * t, 2 * t + 1):
            at = pl.ds(k * (size // 2), size // 2)
            part = Part(
                me, orders[k], buf.at[at], inbox.at[at], outb.at[at], size // 2,
                send_sems.at[k], recv_sems.at[k],
            )
            part.start()
            parts.append(part)
        for part in parts[: 2 * t]:
            if part.at == 0:
                part.step()

    back = (zero_row, zero_row, zero_row, zero_row)
    for t in range(3):
        here_t = pl.ds(t * rows, rows)
        slope_ref[here_t] = slope_ref[here_t] * dot_nt(
            sd_ref[...], second_ref[t * channels : (t + 1) * channels]
        )

        def back_block(i, carry, t=t):
            start = pl.multiple_of(i * BLOCK, BLOCK)
            at = pl.ds(pl.multiple_of(t * rows + i * BLOCK, BLOCK), BLOCK)
            delta = slope_ref[at]
            is_b, _ = masks(t, start, BLOCK, channels)
            scaled = delta * norm_ref[at]
            add = [jnp.where(is_b, 0.0, delta), jnp.where(is_b, delta, 0.0)]
            add += [jnp.where(is_b, 0.0, scaled), jnp.where(is_b, scaled, 0.0)]
            return tuple(c + jnp.sum(a, axis=0, keepdims=True) for c, a in zip(carry, add))

        back = lax.fori_loop(0, rows // BLOCK, back_block, back)
        if t < 2:
            for part in parts[4 - 4 * t :]:
                part.step()
    acc = [by_tap(slope_ref, t) for t in range(3)]

    grad_a = jnp.zeros((TAPS, channels), F32)
    for t in range(3):
        grad_a = grad_a + rstd_a * acc[t][5 * t : 5 * t + TAPS]
        grad_a = grad_a + rstd_b * acc[t][32 + 5 * t : 32 + 5 * t + TAPS]
    erow[0:TAPS] = grad_a
    one = spread(back[0], back[1])
    two = spread(back[2], back[3])
    erow[16:24] = jnp.concatenate(one + two, axis=0)
    norm_a = rstd_a * (pre_a - w_a * mean_a)
    norm_b = rstd_b * (pre_b - w_b * mean_b)
    for u, value in enumerate(spread(norm_a, norm_b)):
        erow[24 + u * TAPS : 24 + (u + 1) * TAPS] = value
    erow[10:16] = jnp.zeros((6, channels), F32)
    for u, w in enumerate(spread(w_rows[0:1], w_rows[1:2])):
        erow[10 + u : 11 + u, 0:128] = w
    high = erow.shape[0] // 8
    for c in range(blocks):
        ex[c * high : (c + 1) * high] = erow[:, c * 128 : (c + 1) * 128].reshape(high, 8, 128)
    extra = Part(
        me, orders[6], ex, ex_in, ex_out, blocks * high, send_sems.at[6], recv_sems.at[6]
    )
    extra.start()
    for turn in range(2 * bits):
        for i, part in enumerate(parts):
            if part.at < 2 * bits:
                part.step()
            if i == len(parts) // 2 - 1 and turn < 4 and extra.at < 2 * bits:
                extra.step()
        if extra.at < 2 * bits:
            extra.step()
    for c in range(blocks):
        erow[:, c * 128 : (c + 1) * 128] = ex_out[c * high : (c + 1) * high].reshape(8 * high, 128)
    weights, scales = [], []
    result = erow[0:TAPS]
    for u in range(utts):
        weights.append(erow[10 + u : 11 + u, 0:128])
        scales.append(rstds[u] * (erow[16 + u : 17 + u] / counts[u]))
        result = result - rstds[u] * (erow[16 + utts + u : 17 + utts + u] / counts[u]) * (
            erow[24 + u * TAPS : 24 + (u + 1) * TAPS]
        )
    pad = [jnp.zeros((8 - utts, 128), F32)], [jnp.zeros((8 - utts, channels), F32)]
    plain = dot_tn(
        jnp.concatenate(weights + pad[0], axis=0), jnp.concatenate(scales + pad[1], axis=0), HIGH
    )
    grad1_ref[...] = (result - plain[0:TAPS] - plain[32 : 32 + TAPS]) * factor
    halo.wait_send()
    for copy in stat_copies:
        copy.wait_send()
    for part in parts + [extra]:
        part.drain()


def finish(factor, feat_in, grad1_in, tiled_ref, feat_ref, grad1_ref, grad2_ref):
    feat_ref[...] = feat_in[...]
    grad1_ref[...] = grad1_in[...]
    grad2_ref[...] = tiled_ref[...].reshape(grad2_ref.shape) * factor


def on_device(waveform, lengths, conv_first, conv_second, cotangent):
    n = lax.axis_size("seq")
    samples = waveform[0]
    rows = samples.shape[0] // TAPS
    channels = conv_second.shape[1]
    utts = lengths.shape[1]
    assert 24 + utts * TAPS <= 64 and utts == 4 and samples.shape[0] < MIN_UNITS * 640
    count = 3 * rows
    table = jnp.pad(waveform[0], (0, 8 * TAPS)).reshape(rows + 8, TAPS)
    factor = float(lax.axis_size("dp") * rows * n) ** (-0.5)
    tiles = 3 * channels // 8 * (channels // 128)
    small = 64 // 8 * (channels // 128)
    bits = n.bit_length() - 1
    vmem = pl.BlockSpec(memory_space=pltpu.VMEM)
    feats, grad1, tiled = pl.pallas_call(
        functools.partial(kernel, n, factor),
        name="encoder",
        out_shape=(
            jax.ShapeDtypeStruct((rows, channels), jnp.bfloat16),
            jax.ShapeDtypeStruct((TAPS, channels), F32),
            jax.ShapeDtypeStruct((tiles, 8, 128), F32),
        ),
        in_specs=[pl.BlockSpec(memory_space=pltpu.SMEM)] + [vmem] * 4,
        out_specs=(vmem, vmem, vmem),
        scratch_shapes=[
            pltpu.VMEM((rows + 8, 128), F32),
            pltpu.VMEM((8, 128), F32),
            pltpu.VMEM((rows, 128), F32),
            pltpu.VMEM((3 * 128, channels), F32),
            pltpu.VMEM((count, channels), F32),
            pltpu.VMEM((count, channels), F32),
            pltpu.VMEM((count, 128), F32),
            pltpu.VMEM((count, channels), jnp.bfloat16),
            pltpu.VMEM((rows, channels), jnp.bfloat16),
            pltpu.VMEM((8, 2 * utts, channels), F32),
            pltpu.VMEM((max(1, n // 8), 2 * utts, channels), F32),
            pltpu.VMEM((tiles, 8, 128), F32),
            pltpu.VMEM((tiles, 8, 128), F32),
            pltpu.VMEM((small, 8, 128), F32),
            pltpu.VMEM((small, 8, 128), F32),
            pltpu.VMEM((small, 8, 128), F32),
            pltpu.VMEM((64, channels), F32),
            pltpu.SemaphoreType.DMA((7, 2 * bits)),
            pltpu.SemaphoreType.DMA((7, 2 * bits)),
            pltpu.SemaphoreType.DMA((8 + n // 8,)),
            pltpu.SemaphoreType.DMA((8 + n // 8,)),
            pltpu.SemaphoreType.DMA((2,)),
        ],
        compiler_params=pltpu.CompilerParams(
            collective_id=0, has_side_effects=True, vmem_limit_bytes=60 * 1024 * 1024
        ),
    )(lengths, table, conv_first, conv_second, cotangent[0])
    cols = channels // 128
    feats, grad1, grad2 = pl.pallas_call(
        functools.partial(finish, factor),
        name="finish",
        grid=(cols,),
        out_shape=(
            jax.ShapeDtypeStruct((rows, channels), jnp.bfloat16),
            jax.ShapeDtypeStruct((TAPS, channels), F32),
            jax.ShapeDtypeStruct((3 * channels, channels), F32),
        ),
        in_specs=[
            pl.BlockSpec((rows // cols, channels), lambda i: (i, 0)),
            pl.BlockSpec((TAPS, 128), lambda i: (0, i)),
            pl.BlockSpec((3, 1, channels // 8, 8, 128), lambda i: (0, i, 0, 0, 0)),
        ],
        out_specs=(
            pl.BlockSpec((rows // cols, channels), lambda i: (i, 0)),
            pl.BlockSpec((TAPS, 128), lambda i: (0, i)),
            pl.BlockSpec((3 * channels, 128), lambda i: (0, i)),
        ),
    )(feats, grad1, tiled.reshape(3, cols, channels // 8, 8, 128))
    if lax.axis_size("dp") > 1:
        grad1, grad2 = lax.psum((grad1, grad2), "dp")
    return (feats[None], grad1, grad2)


def solution(mesh):
    placed = (P("dp", "seq"), P("dp", None), P(), P(), P("dp", "seq", None))
    return jax.shard_map(
        on_device,
        mesh=mesh,
        in_specs=placed,
        out_specs=(P("dp", "seq", None), P(), P()),
        check_vma=False,
    )
```
